32 devices in a mesh: groups: 2 (over x), zonal: 16 (over z, y, core).
Axes of the slice: x: 2, y: 2, z: 4, core: 2. Of those that a mesh axis runs over, the one named last changes fastest.
Arguments:
- field: bfloat16 [192, 32, 2048], P('groups', None, 'zonal'), parts along dimension 0, may hold values from -6 to 6
- land_mask: int32 [32, 2048], P(None, 'zonal'), may hold values from 0 to 1, as said below
- dw_weight: float32 [2, 49, 96], replicated, may hold values from -0.875 to 0.875
- ln_gain: float32 [2, 96], replicated, may hold values from 0.1 to 1.9
- ln_shift: float32 [2, 96], replicated, may hold values from -3 to 3
- w_in: bfloat16 [2, 384, 96], replicated, may hold values from -0.625 to 0.625
- b_in: float32 [2, 384], replicated, may hold values from -3 to 3
- w_out: bfloat16 [2, 96, 384], replicated, may hold values from -0.3125 to 0.3125
Outputs:
- evolved: bfloat16 [192, 32, 2048], P('groups', None, 'zonal'), parts along dimension 0
The draws below stay inside these ranges and needn't reach their ends.
There are 2 independent parts, one for each index of `groups`. The reference program is written for one: setup_inputs(seed, part) draws one part's arguments, and reference() takes and returns one part's arrays. A program takes and returns all parts, laid end to end along the dimension named above; an argument that names none is the same for every part. Nothing has to cross between parts.
Inputs may be any that keep to these rules, and one draw needn't show every extreme that they name: `land_mask`: 1 marks an ocean cell, 0 a land cell.
All inputs are finite; a program needn't handle non-finite values.
Results may differ from the reference program's by a relative error of at most 0.0058.
Values may be sent and summed in bfloat16 or wider, within the bound.
A program may use at most 64 MiB of HBM per device.

```python
import jax
import jax.numpy as jnp
from jax import lax

C = 96
H = 384
BLOCKS = 2
ROWS = 32
CX = 128
NX = 2048


def draw_land_mask(key, part):
    key_tile = jax.random.fold_in(key, 11)
    key_cell = jax.random.fold_in(key, 23)
    tile_land = jax.random.randint(key_tile, (ROWS // 32, NX // CX), 0, 3) == 0
    cell_land = jax.random.randint(key_cell, (ROWS, NX), 0, 8) == 0
    blocks = jnp.repeat(jnp.repeat(tile_land, 32, axis=0), CX, axis=1)
    ocean = jnp.logical_not(jnp.logical_or(blocks, cell_land))
    return ocean.astype(jnp.int32)


def steps_of(rng, dims, cuts, low, top_value):
    def one(dim, shards_of):
        heights = jax.random.uniform(jax.random.fold_in(jax.random.fold_in(rng, 6), dim), (shards_of,), jnp.float32, low / len(cuts), top_value / len(cuts))
        return jnp.repeat(jnp.exp(heights), dims[dim] // shards_of).reshape((-1,) + (1,) * (len(dims) - dim - 1))

    level = one(*cuts[0])
    for cut in cuts[1:]:
        level = level * one(*cut)
    return level


def centred(own_key, extent, spread, bound, split=(), kind=jnp.bfloat16):
    entries = spread * jax.random.normal(own_key, extent, jnp.float32)
    if split:
        entries = entries * steps_of(own_key, extent, split, -0.22, 0.18)
    return jnp.clip(entries, -bound, bound).astype(kind)


def setup_inputs(seed: int = 0, part: int = 0) -> dict:
    key_list = jax.random.split(jax.random.key(seed), 9)
    own_keys = jax.random.split(jax.random.fold_in(key_list[8], part), 9)
    field = centred(own_keys[0], (C, ROWS, NX), 1.0, 6.0, ((2, 16),))
    land_mask = draw_land_mask(jax.random.fold_in(key_list[8], 71), part)
    dw_weight = centred(key_list[2], (BLOCKS, 49, C), 49 ** -0.5, 0.875, (), jnp.float32)
    ln_gain = jnp.clip(1.0 + 0.18 * jax.random.normal(key_list[3], (BLOCKS, C), jnp.float32), 0.1, 1.9)
    ln_shift = centred(key_list[4], (BLOCKS, C), 0.5, 3.0, (), jnp.float32)
    w_in = centred(key_list[5], (BLOCKS, H, C), C ** -0.5, 0.625)
    b_in = centred(key_list[6], (BLOCKS, H), 0.5, 3.0, (), jnp.float32)
    w_out = centred(key_list[7], (BLOCKS, C, H), H ** -0.5, 0.3125)
    return {"field": field, "land_mask": land_mask, "dw_weight": dw_weight, "ln_gain": ln_gain, "ln_shift": ln_shift, "w_in": w_in, "b_in": b_in, "w_out": w_out}


def pad_state(state):
    ext = jnp.concatenate([state[:, :, -3:], state, state[:, :, :3]], axis=2)
    north = ext[:, -3:, ::-1][:, ::-1, :]
    south = jnp.zeros((state.shape[0], 3, ext.shape[2]), state.dtype)
    return jnp.concatenate([south, ext, north], axis=1)

def reference(field, land_mask, dw_weight, ln_gain, ln_shift, w_in, b_in, w_out):
    mask_b = land_mask.astype(jnp.bfloat16)
    state = field * mask_b[None]
    for blk in range(BLOCKS):
        padded = pad_state(state)
        conv = jnp.zeros(state.shape, jnp.float32)
        for p in range(7):
            for q in range(7):
                conv = conv + dw_weight[blk, 7 * p + q][:, None, None] * padded[:, p:p + ROWS, q:q + NX]
        gain = ln_gain[blk]
        shift = ln_shift[blk]
        wa = w_in[blk]
        ba = b_in[blk]
        wb = w_out[blk]

        def rowblock(index, out):
            start = (index * 32).astype(jnp.int32)
            yb = lax.dynamic_slice_in_dim(conv, start, 32, 1)
            xb = lax.dynamic_slice_in_dim(state, start, 32, 1)
            mb = lax.dynamic_slice_in_dim(land_mask, start, 32, 0)
            mean = lax.optimization_barrier(jnp.mean(yb, axis=0))
            cent = yb - mean
            var = lax.optimization_barrier(jnp.mean(cent * cent, axis=0))
            normed = (cent * lax.rsqrt(var + 1e-06) * gain[:, None, None] + shift[:, None, None]).astype(jnp.bfloat16)
            flat = normed.reshape(normed.shape[0], -1)
            hidden = jnp.dot(wa, flat, preferred_element_type=jnp.float32) + ba[:, None]
            hidden = jax.nn.gelu(hidden, approximate=True).astype(jnp.bfloat16)
            outer = jnp.dot(wb, hidden, preferred_element_type=jnp.float32).reshape(yb.shape)
            res = (mb.astype(jnp.float32)[None] * (xb.astype(jnp.float32) + outer)).astype(jnp.bfloat16)
            return lax.dynamic_update_slice_in_dim(out, res, start, 1)
        state = lax.fori_loop(0, ROWS // 32, rowblock, jnp.zeros(state.shape, jnp.bfloat16))
    return state
```

```python
import functools

import jax
import jax.numpy as jnp
from jax import lax
from jax.experimental import pallas as pl
from jax.experimental.pallas import tpu as pltpu
from jax.sharding import PartitionSpec as P

F32 = jnp.float32
BF16 = jnp.bfloat16
GROUP = 8
FOLD = 4


def roll(x, shift):
    return pltpu.roll(x, shift % x.shape[-1], axis=x.ndim - 1)


def lanes_of(shape):
    return lax.broadcasted_iota(jnp.int32, shape, len(shape) - 1)


def shifted(cells, halo, lane, d):
    width = cells.shape[-1]
    if d == 0:
        return cells
    beyond = lane < d if d > 0 else lane >= width + d
    return roll(jnp.where(beyond, halo, cells), -d)


def pack_edges(state, pack_ref, top_ref):
    tiles, rows, width = pack_ref.shape
    groups = width // GROUP
    lane = lanes_of((rows, width))

    @pl.loop(0, tiles)
    def _(tile):
        acc = jnp.zeros((rows, width), F32)
        for g in range(groups):
            cells = state[pl.ds((tile * groups + g) * rows, rows), :]
            inside = (lane >= g * GROUP) & (lane < (g + 1) * GROUP)
            acc = jnp.where(inside, roll(cells, g * GROUP + 3), acc)
        pack_ref[tile] = acc.astype(BF16)

    channels = top_ref.shape[1]
    for k in range(3):
        top_ref[k] = state[pl.ds(rows - 1 - k, channels, stride=rows), :].astype(BF16)


def start_kernel(field_ref, mask_ref, pack_ref, top_ref, state):
    channels, rows, width = field_ref.shape
    mask = mask_ref[...].astype(F32)

    @pl.loop(0, channels)
    def _(c):
        state[pl.ds(c * rows, rows), :] = field_ref[c].astype(F32) * mask

    pack_edges(state, pack_ref, top_ref)


def exchange_kernel(n, pack_ref, top_ref, west, east, ftop, feast, fwest, send, recv):
    me = lax.axis_index("zonal")
    rows = pack_ref.shape[1]
    right, left = lax.rem(me + 1, n), lax.rem(me + n - 1, n)
    across = n - 1 - me
    a_east, a_west = lax.rem(across + 1, n), lax.rem(across + n - 1, n)
    barrier = pltpu.get_barrier_semaphore()

    def greet(device):
        pl.semaphore_signal(
            barrier, inc=1, device_id={"zonal": device}, device_id_type=pl.DeviceIdType.MESH
        )

    for device in (right, left, across):
        greet(device)

    @pl.when(a_east != me)
    def _():
        greet(a_east)

    @pl.when(a_west != me)
    def _():
        greet(a_west)

    alone = jnp.where(a_east == me, 1, 0) + jnp.where(a_west == me, 1, 0)
    pl.semaphore_wait(barrier, 5 - alone)

    def copy(src, dst, slot, device):
        return pltpu.make_async_remote_copy(
            src_ref=src,
            dst_ref=dst,
            send_sem=send.at[slot],
            recv_sem=recv.at[slot],
            device_id={"zonal": device},
            device_id_type=pl.DeviceIdType.MESH,
        )

    edge = pack_ref.at[:, pl.ds(rows // 2, rows // 2), :]
    copies = [
        copy(top_ref, ftop, 2, across),
        copy(pack_ref, west, 0, right),
        copy(pack_ref, east, 1, left),
    ]
    for each in copies:
        each.start()
    for slot, device, dst in ((3, a_east, feast), (4, a_west, fwest)):

        @pl.when(device != me)
        def _():
            copy(edge, dst, slot, device).start()

        @pl.when(device == me)
        def _():
            pltpu.make_async_copy(edge, dst, recv.at[slot]).start()

    for slot, device, dst in ((3, a_east, feast), (4, a_west, fwest)):

        @pl.when(device != me)
        def _():
            copy(edge, dst, slot, device).wait()

        @pl.when(device == me)
        def _():
            pltpu.make_async_copy(edge, dst, recv.at[slot]).wait()

    for each in copies:
        each.wait()


def block_kernel(
    block, last, step, state_ref, mask_ref, west, east, ftop, feast, fwest, dw_ref, gain_ref,
    shift_ref, wa_ref, ba_ref, wb_ref, out_ref, *rest,
):
    pack_ref, top_ref = (None, None) if last else rest[:2]
    state, conv, t_low, t_high, north_halo, north = rest[-6:]
    channels, rows, width = state_ref.shape
    tiles = west.shape[0]
    groups = width // GROUP
    taps = dw_ref.shape[1]
    hidden_units = wa_ref.shape[1]
    lane = lanes_of((rows, width))
    maskf = mask_ref[...].astype(F32)

    tap = lax.broadcasted_iota(jnp.int32, (taps, 2 * width), 0)
    col = lax.broadcasted_iota(jnp.int32, (taps, 2 * width), 1)
    p, q = tap // 7, tap % 7
    main = 7 * rows
    beyond = col - main
    hit = jnp.where(
        col < main,
        jnp.where(col // rows == q, col % rows + 3 - p, -1),
        jnp.where(
            (beyond // FOLD == q) & (beyond % FOLD < 3), rows + 3 + beyond % FOLD - p, -1
        ),
    )
    weights = jnp.transpose(dw_ref[block]).astype(BF16)
    for r in range(rows):
        pick = jnp.where(hit == r, 1.0, 0.0).astype(BF16)
        band = jnp.dot(weights, pick, preferred_element_type=F32)
        t_low[pl.ds(r, channels, stride=rows), :] = band[:, :width]
        t_high[pl.ds(r, channels, stride=rows), :] = band[:, width:]

    half = rows // 2
    lane_half = lanes_of((half, width))

    @pl.loop(0, tiles)
    def _(tile):
        both = jnp.where(
            lane_half % GROUP >= 3, feast[tile].astype(F32), fwest[tile].astype(F32)
        )
        for g in range(groups):
            north_halo[pl.ds((tile * groups + g) * half, half), :] = roll(both, -(g * GROUP + 3))

    north[...] = jnp.zeros_like(north)
    flip = jnp.where(
        lax.broadcasted_iota(jnp.int32, (width, width), 0) + lanes_of((width, width)) == width - 1,
        1.0,
        0.0,
    ).astype(BF16)
    lane_c = lanes_of((channels, width))
    for k in range(3):
        halo = north_halo[pl.ds(half - 1 - k, channels, stride=half), :].astype(BF16)
        halo = jnp.dot(halo, flip, preferred_element_type=F32)
        cells = jnp.dot(ftop[k], flip, preferred_element_type=F32)
        for j in range(7):
            north[pl.ds(j * FOLD + k, channels, stride=rows), :] = shifted(
                cells, halo, lane_c, j - 3
            )

    @pl.loop(0, tiles)
    def _(tile):
        both = jnp.where(lane % GROUP >= 3, east[tile].astype(F32), west[tile].astype(F32))
        for g in range(groups):
            c = tile * groups + g
            at = pl.ds(c * rows, rows)
            cells = state_ref[c].astype(F32) * maskf
            state[at, :] = cells
            halo = roll(both, -(g * GROUP + 3))
            parts = [shifted(cells, halo, lane, j - 3).astype(BF16) for j in range(7)]
            parts.append(north[at, :].astype(BF16))
            band = jnp.concatenate([t_low[at, :], t_high[at, :]], axis=1).astype(BF16)
            conv[at, :] = jnp.dot(
                band, jnp.concatenate(parts, axis=0), preferred_element_type=F32
            )

    gain = jnp.transpose(jnp.broadcast_to(gain_ref[block : block + 1], (width, channels)))
    shift = jnp.transpose(jnp.broadcast_to(shift_ref[block : block + 1], (width, channels)))
    bias = jnp.transpose(jnp.broadcast_to(ba_ref[block : block + 1], (width, hidden_units)))
    bias = jnp.concatenate([bias] * step, axis=1)
    wa, wb = wa_ref[block], wb_ref[block]

    @pl.loop(0, rows // step)
    def _(index):
        normed = []
        for k in range(step):
            y = conv[pl.ds(index * step + k, channels, stride=rows), :]
            mean = jnp.sum(y, axis=0, keepdims=True) * (1.0 / channels)
            cent = y - mean
            var = jnp.sum(cent * cent, axis=0, keepdims=True) * (1.0 / channels)
            normed.append((cent * lax.rsqrt(var + 1e-06) * gain + shift).astype(BF16))
        v = jnp.dot(wa, jnp.concatenate(normed, axis=1), preferred_element_type=F32) + bias
        k0 = 0.7978845608028654
        th = jnp.tanh(v * (k0 + (k0 * 0.044715) * (v * v)))
        twice = (v + v * th).astype(BF16)
        outer = 0.5 * jnp.dot(wb, twice, preferred_element_type=F32)
        for k in range(step):
            at = pl.ds(index * step + k, channels, stride=rows)
            keep = mask_ref[pl.ds(index * step + k, 1), :].astype(F32)
            res = keep * (state[at, :] + outer[:, k * width : (k + 1) * width])
            state[at, :] = res.astype(BF16).astype(F32)

    @pl.loop(0, channels)
    def _(c):
        out_ref[c] = state[pl.ds(c * rows, rows), :].astype(BF16)

    if not last:
        pack_edges(state, pack_ref, top_ref)


VMEM = pl.BlockSpec(memory_space=pltpu.VMEM)
LIMIT = 56 * 1024 * 1024


def local(field, land_mask, dw_weight, ln_gain, ln_shift, w_in, b_in, w_out):
    channels, rows, width = field.shape
    blocks = dw_weight.shape[0]
    n = lax.axis_size("zonal")
    tiles = channels * GROUP // width
    packed = (
        jax.ShapeDtypeStruct((tiles, rows, width), BF16),
        jax.ShapeDtypeStruct((3, channels, width), BF16),
    )
    half = jax.ShapeDtypeStruct((tiles, rows // 2, width), BF16)
    flat = pltpu.VMEM((channels * rows, width), F32)
    pack, top = pl.pallas_call(
        start_kernel,
        out_shape=packed,
        in_specs=[VMEM] * 2,
        out_specs=(VMEM,) * 2,
        scratch_shapes=[flat],
        compiler_params=pltpu.CompilerParams(vmem_limit_bytes=LIMIT),
        name="start",
    )(field, land_mask)
    state = field
    for block in range(blocks):
        last = block == blocks - 1
        halos = pl.pallas_call(
            functools.partial(exchange_kernel, n),
            out_shape=(packed[0], packed[0], packed[1], half, half),
            in_specs=[VMEM] * 2,
            out_specs=(VMEM,) * 5,
            scratch_shapes=[pltpu.SemaphoreType.DMA((5,)), pltpu.SemaphoreType.DMA((5,))],
            compiler_params=pltpu.CompilerParams(collective_id=block, has_side_effects=True),
            name=f"exchange{block}",
        )(pack, top)
        outs = (jax.ShapeDtypeStruct(field.shape, BF16),) + (() if last else packed)
        res = pl.pallas_call(
            functools.partial(block_kernel, block, last, 4),
            out_shape=outs,
            in_specs=[VMEM] * 13,
            out_specs=(VMEM,) * len(outs),
            scratch_shapes=[
                flat,
                flat,
                flat,
                flat,
                pltpu.VMEM((channels * rows // 2, width), F32),
                flat,
            ],
            compiler_params=pltpu.CompilerParams(vmem_limit_bytes=LIMIT),
            name=f"block{block}",
        )(state, land_mask, *halos, dw_weight, ln_gain, ln_shift, w_in, b_in, w_out)
        state = res[0]
        if not last:
            pack, top = res[1:]
    return state


def solution(mesh):
    placed = (P("groups", None, "zonal"), P(None, "zonal"), P(), P(), P(), P(), P(), P())
    return jax.shard_map(
        local, mesh=mesh, in_specs=placed, out_specs=P("groups", None, "zonal"), check_vma=False
    )
```

```python
import functools

import jax
import jax.numpy as jnp
from jax import lax
from jax.experimental import pallas as pl
from jax.experimental.pallas import tpu as pltpu
from jax.sharding import PartitionSpec as P

F32 = jnp.float32
BF16 = jnp.bfloat16
GROUP = 8
FOLD = 6
TAIL = 4
STEP = 14
PAD = 1


def roll(x, shift):
    return pltpu.roll(x, shift % x.shape[-1], axis=x.ndim - 1)


def lanes_of(shape):
    return lax.broadcasted_iota(jnp.int32, shape, len(shape) - 1)


def shifted(cells, halo, lane, d):
    width = cells.shape[-1]
    if d == 0:
        return cells
    beyond = lane < d if d > 0 else lane >= width + d
    return roll(jnp.where(beyond, halo, cells), -d)


def kernel(
    n, field_ref, mask_ref, dw_ref, gain_ref, shift_ref, wa_ref, ba_ref, wb_ref, out_ref, state,
    conv, t_low, t_high, pack, top, edge, west, east, ftop, feast, fwest, expand,
    send, recv,
):
    channels, rows, width = field_ref.shape
    taps, blocks = dw_ref.shape[:2]
    hidden_units = wa_ref.shape[2]
    tiles = pack.shape[1]
    groups = width // GROUP
    deep = edge.shape[1]
    pitch = rows + PAD
    lane = lanes_of((rows, width))
    lane_c = lanes_of((channels, width))
    lane_e = lanes_of((deep, width))
    maskf = mask_ref[...].astype(F32)

    me = lax.axis_index("zonal")
    right, left = lax.rem(me + 1, n), lax.rem(me + n - 1, n)
    across = n - 1 - me
    a_east, a_west = lax.rem(across + 1, n), lax.rem(across + n - 1, n)
    barrier = pltpu.get_barrier_semaphore()

    def greet(device):
        pl.semaphore_signal(
            barrier, inc=1, device_id={"zonal": device}, device_id_type=pl.DeviceIdType.MESH
        )

    for device in (right, left, across):
        greet(device)

    @pl.when(a_east != me)
    def _():
        greet(a_east)

    @pl.when(a_west != me)
    def _():
        greet(a_west)

    def copy(src, dst, block, slot, device):
        return pltpu.make_async_remote_copy(
            src_ref=src.at[block],
            dst_ref=dst.at[block],
            send_sem=send.at[block, slot],
            recv_sem=recv.at[block, slot],
            device_id={"zonal": device},
            device_id_type=pl.DeviceIdType.MESH,
        )

    def sides(block):
        return copy(pack, west, block, 0, right), copy(pack, east, block, 1, left)

    def fold(block, act):
        for slot, device, dst in ((3, a_east, feast), (4, a_west, fwest)):

            @pl.when(device != me)
            def _():
                act(copy(edge, dst, block, slot, device))

            @pl.when(device == me)
            def _():
                act(
                    pltpu.make_async_copy(
                        edge.at[block], dst.at[block], recv.at[block, slot]
                    )
                )

        act(copy(top, ftop, block, 2, across))

    def row(r):
        return pl.ds(r, channels, stride=pitch)

    def pack_top(block):
        acc = jnp.zeros((deep, width), F32)
        for k in range(3):
            cells = state[row(rows - 1 - k), :]
            top[block, k] = cells.astype(BF16)
            for part in range(channels // deep):
                at = (k * (channels // deep) + part) * FOLD
                inside = (lane_e >= at) & (lane_e < at + FOLD)
                acc = jnp.where(inside, roll(cells[part * deep : (part + 1) * deep], at + 3), acc)
        edge[block] = acc.astype(BF16)

    def pack_side(block, tile, each):
        acc = jnp.zeros((rows, width), F32)
        for g in range(groups):
            inside = (lane >= g * GROUP) & (lane < (g + 1) * GROUP)
            acc = jnp.where(inside, roll(each(tile * groups + g), g * GROUP + 3), acc)
        pack[block, tile] = acc.astype(BF16)

    def send_all(block):
        for each in sides(block):
            each.start()
        fold(block, lambda c: c.start())

    def bands(weights):
        tap = lax.broadcasted_iota(jnp.int32, (taps, 2 * width), 0)
        col = lax.broadcasted_iota(jnp.int32, (taps, 2 * width), 1)
        p, q = tap // 7, tap % 7
        hit = jnp.where(col // rows == q, col % rows + 3 - p, -1)
        weights = weights.astype(BF16)
        for r in range(rows):
            pick = jnp.where(hit == r, 1.0, 0.0).astype(BF16)
            band = jnp.dot(weights, pick, preferred_element_type=F32)
            t_low[row(r), :] = band[:, :width]
            t_high[row(r), :] = band[:, width:]

    def add_north(block, weights):
        flip = jnp.where(
            lax.broadcasted_iota(jnp.int32, (width, width), 0) + lanes_of((width, width))
            == width - 1,
            1.0,
            0.0,
        ).astype(BF16)
        both = jnp.where(
            lane_e % FOLD >= 3, feast[block].astype(F32), fwest[block].astype(F32)
        )
        sums = [conv[row(rows - 3 + r), :] for r in range(3)]
        for k in range(3):
            parts = [
                roll(both, -((k * (channels // deep) + part) * FOLD + 3))
                for part in range(channels // deep)
            ]
            halo = jnp.dot(
                jnp.concatenate(parts, axis=0).astype(BF16), flip, preferred_element_type=F32
            )
            cells = jnp.dot(ftop[block, k], flip, preferred_element_type=F32)
            for q in range(7):
                moved = shifted(cells, halo, lane_c, q - 3)
                for r in range(k, 3):
                    at = 7 * (6 + k - r) + q
                    sums[r] = sums[r] + weights[:, at : at + 1] * moved
        for r in range(3):
            conv[row(rows - 3 + r), :] = sums[r]

    def all_columns(ref, block, size):
        return jnp.transpose(jnp.broadcast_to(ref[block : block + 1], (width, size)))

    def mlp(block, start, step):
        gain = all_columns(gain_ref, block, channels)
        shift = all_columns(shift_ref, block, channels)
        bias = jnp.concatenate([all_columns(ba_ref, block, hidden_units)] * step, axis=1)
        normed = []
        for k in range(step):
            y = conv[row(start + k), :]
            mean = jnp.sum(y, axis=0, keepdims=True) * (1.0 / channels)
            cent = y - mean
            var = jnp.sum(cent * cent, axis=0, keepdims=True) * (1.0 / channels)
            normed.append((cent * lax.rsqrt(var + 1e-06) * gain + shift).astype(BF16))
        v = jnp.dot(
            expand[block], jnp.concatenate(normed, axis=1), preferred_element_type=F32
        )
        v = v + bias
        k0 = 0.7978845608028654
        th = jnp.tanh(v * (k0 + (k0 * 0.044715) * (v * v)))
        twice = (v + v * th).astype(BF16)
        outer = 0.5 * jnp.dot(wb_ref[block], twice, preferred_element_type=F32)
        for k in range(step):
            keep = mask_ref[pl.ds(start + k, 1), :].astype(F32)
            res = keep * (state[row(start + k), :] + outer[:, k * width : (k + 1) * width])
            state[row(start + k), :] = res.astype(BF16).astype(F32)

    @pl.loop(0, tiles)
    def _(tile):
        def masked(c):
            cells = field_ref[c].astype(F32) * maskf
            state[pl.ds(c * pitch, rows), :] = cells
            return cells

        pack_side(0, tile, masked)

    pack_top(0)
    alone = jnp.where(a_east == me, 1, 0) + jnp.where(a_west == me, 1, 0)
    pl.semaphore_wait(barrier, 5 - alone)
    send_all(0)

    for block in range(blocks):
        weights = jnp.transpose(dw_ref[:, block, :])
        expand[block] = jnp.transpose(wa_ref[block])
        bands(weights)
        for each in sides(block):
            each.wait()

        @pl.loop(0, tiles)
        def _(tile):
            both = jnp.where(
                lane % GROUP >= 3, east[block, tile].astype(F32), west[block, tile].astype(F32)
            )
            for g in range(groups):
                c = tile * groups + g
                at = pl.ds(c * pitch, rows)
                cells = state[at, :]
                halo = roll(both, -(g * GROUP + 3))
                parts = [shifted(cells, halo, lane, j - 3).astype(BF16) for j in range(7)]
                band = jnp.concatenate([t_low[at, :], t_high[at, :]], axis=1).astype(BF16)
                conv[at, :] = jnp.dot(
                    band[:, : 7 * rows],
                    jnp.concatenate(parts, axis=0),
                    preferred_element_type=F32,
                )

        @pl.loop(0, (rows - TAIL) // STEP)
        def _(index):
            mlp(block, index * STEP, STEP)

        fold(block, lambda c: c.wait())
        add_north(block, weights)
        mlp(block, rows - TAIL, TAIL)

        if block < blocks - 1:

            @pl.loop(0, tiles)
            def _(tile):
                pack_side(block + 1, tile, lambda c: state[pl.ds(c * pitch, rows), :])

            pack_top(block + 1)
            send_all(block + 1)

    @pl.loop(0, channels)
    def _(c):
        out_ref[c] = state[pl.ds(c * pitch, rows), :].astype(BF16)


VMEM = pl.BlockSpec(memory_space=pltpu.VMEM)


def local(field, land_mask, dw_weight, ln_gain, ln_shift, w_in, b_in, w_out):
    channels, rows, width = field.shape
    blocks = dw_weight.shape[0]
    tiles = channels * GROUP // width
    flat = pltpu.VMEM((channels * (rows + PAD), width), F32)
    packed = pltpu.VMEM((blocks, tiles, rows, width), BF16)
    tops = pltpu.VMEM((blocks, 3, channels, width), BF16)
    edges = pltpu.VMEM((blocks, 16, width), BF16)
    return pl.pallas_call(
        functools.partial(kernel, lax.axis_size("zonal")),
        out_shape=jax.ShapeDtypeStruct(field.shape, BF16),
        in_specs=[VMEM] * 8,
        out_specs=VMEM,
        scratch_shapes=[
            flat,
            flat,
            flat,
            flat,
            packed,
            tops,
            edges,
            packed,
            packed,
            tops,
            edges,
            edges,
            pltpu.VMEM(w_in.shape, BF16),
            pltpu.SemaphoreType.DMA((blocks, 5)),
            pltpu.SemaphoreType.DMA((blocks, 5)),
        ],
        compiler_params=pltpu.CompilerParams(
            collective_id=0, has_side_effects=True, vmem_limit_bytes=56 * 1024 * 1024
        ),
        name="evolve",
    )(
        field,
        land_mask,
        jnp.swapaxes(dw_weight, 0, 1),
        ln_gain,
        ln_shift,
        jnp.swapaxes(w_in, 1, 2),
        b_in,
        w_out,
    )


def solution(mesh):
    placed = (P("groups", None, "zonal"), P(None, "zonal"), P(), P(), P(), P(), P(), P())
    return jax.shard_map(
        local, mesh=mesh, in_specs=placed, out_specs=P("groups", None, "zonal"), check_vma=False
    )
```

```python
import functools

import jax
import jax.numpy as jnp
from jax import lax
from jax.experimental import pallas as pl
from jax.experimental.pallas import tpu as pltpu
from jax.sharding import PartitionSpec as P

F32 = jnp.float32
BF16 = jnp.bfloat16
GROUP = 8
FOLD = 6
TAIL = 4
STEP = 28
PAD = 4


def roll(x, shift):
    return pltpu.roll(x, shift % x.shape[-1], axis=x.ndim - 1)


def lanes_of(shape):
    return lax.broadcasted_iota(jnp.int32, shape, len(shape) - 1)


def shifted(cells, halo, lane, d):
    width = cells.shape[-1]
    if d == 0:
        return cells
    beyond = lane < d if d > 0 else lane >= width + d
    return roll(jnp.where(beyond, halo, cells), -d)


def kernel(
    n, field_ref, mask_ref, dw_ref, gain_ref, shift_ref, wa_ref, ba_ref, wb_ref, out_ref, state,
    conv, t_low, t_high, pack, top, edge, west, east, ftop, feast, fwest, expand,
    send, recv,
):
    channels, rows, width = field_ref.shape
    taps, blocks = dw_ref.shape[:2]
    hidden_units = wa_ref.shape[2]
    tiles = pack.shape[1]
    groups = width // GROUP
    deep = edge.shape[1]
    pitch = rows + PAD
    half = rows // 2
    lane_h = lanes_of((half, width))
    lane = lanes_of((rows, width))
    lane_c = lanes_of((channels, width))
    lane_e = lanes_of((deep, width))
    maskf = mask_ref[...].astype(F32)

    me = lax.axis_index("zonal")
    right, left = lax.rem(me + 1, n), lax.rem(me + n - 1, n)
    across = n - 1 - me
    a_east, a_west = lax.rem(across + 1, n), lax.rem(across + n - 1, n)
    barrier = pltpu.get_barrier_semaphore()

    def greet(device):
        pl.semaphore_signal(
            barrier, inc=1, device_id={"zonal": device}, device_id_type=pl.DeviceIdType.MESH
        )

    for device in (right, left, across):
        greet(device)

    @pl.when(a_east != me)
    def _():
        greet(a_east)

    @pl.when(a_west != me)
    def _():
        greet(a_west)

    def copy(src, dst, block, slot, device):
        return pltpu.make_async_remote_copy(
            src_ref=src.at[block],
            dst_ref=dst.at[block],
            send_sem=send.at[block, slot],
            recv_sem=recv.at[block, slot],
            device_id={"zonal": device},
            device_id_type=pl.DeviceIdType.MESH,
        )

    def sides(block, part):
        part_rows = pl.ds(part * half, half)
        return [
            pltpu.make_async_remote_copy(
                src_ref=pack.at[block, :, part_rows, :],
                dst_ref=dst.at[block, :, part_rows, :],
                send_sem=send.at[block, slot],
                recv_sem=recv.at[block, slot],
                device_id={"zonal": device},
                device_id_type=pl.DeviceIdType.MESH,
            )
            for dst, slot, device in ((west, 5 * part, right), (east, 5 * part + 1, left))
        ]

    def fold(block, act):
        for slot, device, dst in ((3, a_east, feast), (4, a_west, fwest)):

            @pl.when(device != me)
            def _():
                act(copy(edge, dst, block, slot, device))

            @pl.when(device == me)
            def _():
                act(
                    pltpu.make_async_copy(
                        edge.at[block], dst.at[block], recv.at[block, slot]
                    )
                )

        act(copy(top, ftop, block, 2, across))

    def row(r):
        return pl.ds(r, channels, stride=pitch)

    def pack_top(block):
        acc = jnp.zeros((deep, width), F32)
        for k in range(3):
            cells = state[row(rows - 1 - k), :]
            top[block, k] = cells.astype(BF16)
            for part in range(channels // deep):
                at = (k * (channels // deep) + part) * FOLD
                inside = (lane_e >= at) & (lane_e < at + FOLD)
                acc = jnp.where(inside, roll(cells[part * deep : (part + 1) * deep], at + 3), acc)
        edge[block] = acc.astype(BF16)

    def pack_side(block, part):
        @pl.loop(0, tiles)
        def _(tile):
            acc = jnp.zeros((half, width), F32)
            for g in range(groups):
                inside = (lane_h >= g * GROUP) & (lane_h < (g + 1) * GROUP)
                cells = state[pl.ds((tile * groups + g) * pitch + part * half, half), :]
                acc = jnp.where(inside, roll(cells, g * GROUP + 3), acc)
            pack[block, tile, pl.ds(part * half, half), :] = acc.astype(BF16)

    def send_side(block, part):
        for each in sides(block, part):
            each.start()

    def bands(weights):
        tap = lax.broadcasted_iota(jnp.int32, (taps, 2 * width), 0)
        col = lax.broadcasted_iota(jnp.int32, (taps, 2 * width), 1)
        p, q = tap // 7, tap % 7
        hit = jnp.where(col // rows == q, col % rows + 3 - p, -1)
        weights = weights.astype(BF16)
        for r in range(rows):
            pick = jnp.where(hit == r, 1.0, 0.0).astype(BF16)
            band = jnp.dot(weights, pick, preferred_element_type=F32)
            t_low[row(r), :] = band[:, :width]
            t_high[row(r), :] = band[:, width:]

    def add_north(block, weights):
        flip = jnp.where(
            lax.broadcasted_iota(jnp.int32, (width, width), 0) + lanes_of((width, width))
            == width - 1,
            1.0,
            0.0,
        ).astype(BF16)
        both = jnp.where(
            lane_e % FOLD >= 3, feast[block].astype(F32), fwest[block].astype(F32)
        )
        sums = [conv[row(rows - 3 + r), :] for r in range(3)]
        for k in range(3):
            parts = [
                roll(both, -((k * (channels // deep) + part) * FOLD + 3))
                for part in range(channels // deep)
            ]
            halo = jnp.dot(
                jnp.concatenate(parts, axis=0).astype(BF16), flip, preferred_element_type=F32
            )
            cells = jnp.dot(ftop[block, k], flip, preferred_element_type=F32)
            for q in range(7):
                moved = shifted(cells, halo, lane_c, q - 3)
                for r in range(k, 3):
                    at = 7 * (6 + k - r) + q
                    sums[r] = sums[r] + weights[:, at : at + 1] * moved
        for r in range(3):
            conv[row(rows - 3 + r), :] = sums[r]

    def all_columns(ref, block, size):
        return jnp.transpose(jnp.broadcast_to(ref[block : block + 1], (width, size)))

    def mlp(block, start, step):
        gain = all_columns(gain_ref, block, channels)
        shift = all_columns(shift_ref, block, channels)
        bias = jnp.concatenate([all_columns(ba_ref, block, hidden_units)] * step, axis=1)
        normed = []
        for k in range(step):
            y = conv[row(start + k), :]
            mean = jnp.sum(y, axis=0, keepdims=True) * (1.0 / channels)
            cent = y - mean
            var = jnp.sum(cent * cent, axis=0, keepdims=True) * (1.0 / channels)
            normed.append((cent * lax.rsqrt(var + 1e-06) * gain + shift).astype(BF16))
        v = jnp.dot(
            expand[block], jnp.concatenate(normed, axis=1), preferred_element_type=F32
        )
        v = v + bias
        k0 = 0.7978845608028654
        th = jnp.tanh(v * (k0 + (k0 * 0.044715) * (v * v)))
        twice = (v + v * th).astype(BF16)
        outer = 0.5 * jnp.dot(wb_ref[block], twice, preferred_element_type=F32)
        for k in range(step):
            res = state[row(start + k), :] + outer[:, k * width : (k + 1) * width]
            if block < blocks - 1:
                res = mask_ref[pl.ds(start + k, 1), :].astype(F32) * res
            state[row(start + k), :] = res.astype(BF16).astype(F32)

    @pl.loop(0, tiles)
    def _(tile):
        for g in range(groups):
            c = tile * groups + g
            state[pl.ds(c * pitch, rows), :] = field_ref[c].astype(F32) * maskf

    pack_side(0, 0)
    pack_side(0, 1)
    alone = jnp.where(a_east == me, 1, 0) + jnp.where(a_west == me, 1, 0)
    pl.semaphore_wait(barrier, 5 - alone)
    send_side(0, 0)
    send_side(0, 1)
    pack_top(0)
    fold(0, lambda c: c.start())

    for block in range(blocks):
        weights = jnp.transpose(dw_ref[:, block, :])
        expand[block] = jnp.transpose(wa_ref[block])
        bands(weights)
        for each in sides(block, 0) + sides(block, 1):
            each.wait()

        @pl.loop(0, tiles)
        def _(tile):
            both = jnp.where(
                lane % GROUP >= 3, east[block, tile].astype(F32), west[block, tile].astype(F32)
            )
            for g in range(groups):
                c = tile * groups + g
                at = pl.ds(c * pitch, rows)
                cells = state[at, :]
                halo = roll(both, -(g * GROUP + 3))
                parts = [shifted(cells, halo, lane, j - 3).astype(BF16) for j in range(7)]
                band = jnp.concatenate([t_low[at, :], t_high[at, :]], axis=1).astype(BF16)
                conv[at, :] = jnp.dot(
                    band[:, : 7 * rows],
                    jnp.concatenate(parts, axis=0),
                    preferred_element_type=F32,
                )

        @pl.loop(0, (rows - TAIL) // STEP)
        def _(index):
            mlp(block, index * STEP, STEP)

        if block < blocks - 1:
            pack_side(block + 1, 0)
            send_side(block + 1, 0)
        fold(block, lambda c: c.wait())
        add_north(block, weights)
        mlp(block, rows - TAIL, TAIL)

        if block < blocks - 1:
            pack_side(block + 1, 1)
            send_side(block + 1, 1)
            pack_top(block + 1)
            fold(block + 1, lambda c: c.start())

    @pl.loop(0, channels)
    def _(c):
        out_ref[c] = state[pl.ds(c * pitch, rows), :].astype(BF16)


VMEM = pl.BlockSpec(memory_space=pltpu.VMEM)


def local(field, land_mask, dw_weight, ln_gain, ln_shift, w_in, b_in, w_out):
    channels, rows, width = field.shape
    blocks = dw_weight.shape[0]
    tiles = channels * GROUP // width
    flat = pltpu.VMEM((channels * (rows + PAD), width), F32)
    packed = pltpu.VMEM((blocks, tiles, rows, width), BF16)
    tops = pltpu.VMEM((blocks, 3, channels, width), BF16)
    edges = pltpu.VMEM((blocks, 16, width), BF16)
    unmasked = pl.pallas_call(
        functools.partial(kernel, lax.axis_size("zonal")),
        out_shape=jax.ShapeDtypeStruct(field.shape, BF16),
        in_specs=[VMEM] * 8,
        out_specs=VMEM,
        scratch_shapes=[
            flat,
            flat,
            flat,
            flat,
            packed,
            tops,
            edges,
            packed,
            packed,
            tops,
            edges,
            edges,
            pltpu.VMEM(w_in.shape, BF16),
            pltpu.SemaphoreType.DMA((blocks, 7)),
            pltpu.SemaphoreType.DMA((blocks, 7)),
        ],
        compiler_params=pltpu.CompilerParams(
            collective_id=0, has_side_effects=True, vmem_limit_bytes=56 * 1024 * 1024
        ),
        name="evolve",
    )(
        field,
        land_mask,
        jnp.swapaxes(dw_weight, 0, 1),
        ln_gain,
        ln_shift,
        jnp.swapaxes(w_in, 1, 2),
        b_in,
        w_out,
    )
    return unmasked * land_mask.astype(BF16)[None]


def solution(mesh):
    placed = (P("groups", None, "zonal"), P(None, "zonal"), P(), P(), P(), P(), P(), P())
    return jax.shard_map(
        local, mesh=mesh, in_specs=placed, out_specs=P("groups", None, "zonal"), check_vma=False
    )
```
